32 devices in a mesh: dp: 4 (over z), layer: 2 (over x), query: 4 (over y, core).
Axes of the slice: x: 2, y: 2, z: 4, core: 2. Of those that a mesh axis runs over, the one named last changes fastest.
Arguments:
- mantissas: bfloat16 [1024, 2, 4096], P('dp', 'layer'), may hold values from -6 to 6
- exponents: int32 [1024, 2, 32], P('dp', 'layer'), may hold values from -2 to 1
- queries: bfloat16 [1024, 2, 4096], P('query', 'layer'), may hold values from -0.0625 to 0.0625
- doc_ids: int32 [1024], P('dp'), may hold values from 0 to 255, never falling along the last dimension, each value on 1 to 32 neighbouring positions
- owners: int32 [256], replicated, may hold values from 0 to 255, each once
Outputs:
- fisher: float32 [2, 4096, 4096], P('layer', 'dp', 'query')
- doc_scores: float32 [256, 1024], P('dp', 'query')
The draws below stay inside these ranges and needn't reach their ends.
Inputs may be any that keep to these rules, and one draw needn't show every extreme that they name: `doc_ids`: never falling along the rows; every document has 1 to 32 rows, one exactly 32. `owners`: each slot is taken by exactly one document.
All inputs are finite; a program needn't handle non-finite values.
Results may differ from the reference program's by a relative error of at most 0.0003.
Values may be sent and summed in bfloat16 or wider, within the bound.
A program may use at most 64 MiB of HBM per device.

```python
import math
import jax
import jax.numpy as jnp
import numpy as np
from jax import lax

K = 4096
NQ = 1024
MOST = 32
LAYERS = 2
ROWS = 1024
DOCS = 256


def with_ends(array, stream_key, least, largest):
    index_at = [jax.random.randint(jax.random.fold_in(stream_key, axis), (), 0, length) for axis, length in enumerate(array.shape)]
    main_axis = array.shape.index(max(array.shape))
    next_to = index_at[:main_axis] + [(index_at[main_axis] + 1) % array.shape[main_axis]] + index_at[main_axis + 1:]
    return array.at[tuple(index_at)].set(least).at[tuple(next_to)].set(largest)


def steps_of(own_key, extent, cuts, least, high):
    level = 1.0
    for position, parts in cuts:
        steps = jax.random.uniform(jax.random.fold_in(jax.random.fold_in(own_key, 6), position), (parts,), jnp.float32, least / len(cuts), high / len(cuts))
        level = level * jnp.repeat(jnp.exp(steps), extent[position] // parts).reshape((-1,) + (1,) * (len(extent) - 1 - position))
    return level


def split_up(count, total, most, skew):
    portions = [(1 << 20) // math.isqrt(rank ** skew) + 1 for rank in range(2, count + 1)]
    rest, given = total - most - (count - 1), [1] * (count - 1)
    while rest > 0:
        movable = [i for i in range(count - 1) if given[i] < most]
        mass, remaining = sum([portions[i] for i in movable]), rest
        for i in movable:
            more = min(most - given[i], max(1, remaining * portions[i] // mass), rest)
            given[i] = given[i] + more
            rest = rest - more
    return np.array([most] + given)


def ragged_sizes(key, amount, total, bound, slope):
    if amount == 2:
        one = jax.random.randint(key, (), max(1, total - bound), min(bound, total - 1) + 1)
        return jnp.stack([one, total - one])
    tallies = jnp.asarray(split_up(amount, total, bound, slope), jnp.int32)
    pairs = (amount - 1) // 2
    giver, taker = tallies[1:1 + 2 * pairs:2], tallies[2:2 + 2 * pairs:2]
    room = jnp.minimum(giver - 1, bound - taker)
    passed = jax.random.randint(jax.random.fold_in(key, 1), (pairs,), 0, 1 << 20) % (room + 1)
    tallies = tallies.at[1:1 + 2 * pairs:2].set(giver - passed).at[2:2 + 2 * pairs:2].set(taker + passed)
    return tallies[jax.random.permutation(jax.random.fold_in(key, 2), amount)]


def noise(stream_key, extent, spread, most, cuts=(), held_as=jnp.bfloat16):
    drawn = spread * jax.random.normal(stream_key, extent, jnp.float32)
    if cuts:
        drawn = drawn * steps_of(stream_key, extent, cuts, -0.22, 0.18)
    return jnp.clip(drawn, -most, most).astype(held_as)


def setup_inputs(seed: int = 0) -> dict:
    keys = jax.random.split(jax.random.key(seed), 6)
    return {
        "mantissas": noise(keys[0], (ROWS, LAYERS, K), 1.0, 6.0, ((0, 4), (1, 2))),
        "exponents": with_ends(jax.random.randint(keys[1], (ROWS, LAYERS, K // 128), -2, 2), jax.random.fold_in(keys[1], 1), -2, 1).astype(jnp.int32),
        "queries": noise(keys[2], (NQ, LAYERS, K), (LAYERS * K) ** -0.5, 0.0625, ((0, 4), (1, 2))),
        "doc_ids": jnp.searchsorted(jnp.cumsum(ragged_sizes(keys[3], DOCS, ROWS, MOST, 2)), jnp.arange(ROWS), side="right").astype(jnp.int32),
        "owners": jax.random.permutation(keys[4], DOCS).astype(jnp.int32),
    }


def dequant(mantissas, exponents):
    scale = jnp.exp2(exponents.astype(jnp.float32)).astype(jnp.bfloat16)
    rows, layers, width = mantissas.shape
    blocks = mantissas.reshape(rows, layers, width // 128, 128) * scale[..., None]
    return blocks.reshape(rows, layers, width)


def reference(mantissas, exponents, queries, doc_ids, owners):
    grads = dequant(mantissas, exponents)
    rows, layers, width = grads.shape

    def one_layer(slab):
        gram = lax.dot_general(slab, slab, (((0,), (0,)), ((), ())), preferred_element_type=jnp.float32)
        return gram * (1.0 / ROWS)

    fisher = lax.map(one_layer, jnp.transpose(grads, (1, 0, 2)))
    flat_grads = grads.reshape(rows, layers * width)
    flat_queries = queries.reshape(queries.shape[0], layers * width)
    scores = lax.dot_general(flat_grads, flat_queries, (((1,), (1,)), ((), ())), preferred_element_type=jnp.float32)
    slots = owners[doc_ids]
    doc_scores = jax.ops.segment_sum(scores, slots, num_segments=DOCS)
    return fisher, doc_scores
```

```python
import functools

import jax
import jax.numpy as jnp
from jax import lax
from jax.experimental import pallas as pl
from jax.experimental.pallas import tpu as pltpu
from jax.sharding import PartitionSpec as P

MESH = pl.DeviceIdType.MESH
LANES = 128


def remote(src, dst, send, recv, **target):
    return pltpu.make_async_remote_copy(
        src_ref=src, dst_ref=dst, send_sem=send, recv_sem=recv,
        device_id=target, device_id_type=MESH,
    )


def scale_columns(exps):
    return jnp.transpose(jnp.exp2(exps.astype(jnp.float32)))


def spread(scale, width=LANES):
    return jnp.broadcast_to(scale, (scale.shape[0], width)).astype(jnp.bfloat16)


def gather_kernel(
    sizes, m_hbm, e_hbm, q_hbm, doc_ref, owner_ref,
    gcol, gown, ecol, eown, ds_out,
    mv, qv, ev, terms, from_layers, part, from_dp, total,
    load_sem, z_send, z_recv, o_send, o_recv, e_send, e_recv, f_send, f_recv,
    x_send, x_recv, s_send, s_recv, r_send, r_recv, out_sem,
):
    n, layers, queries, pieces, own_width = sizes
    rows, width = m_hbm.shape
    col_width = width // queries
    col_blocks = col_width // LANES
    piece = rows // pieces
    d, l, q = (lax.axis_index(a) for a in ("dp", "layer", "query"))
    source = lax.div(d * own_width, col_width)
    offset = pl.multiple_of(lax.rem(d * own_width, col_width), LANES)
    sub = terms.shape[2]

    def other(index, step, size):
        return lax.rem(index + step + size, size)

    loads = [
        pltpu.make_async_copy(e_hbm, ev, load_sem.at[0]),
        pltpu.make_async_copy(m_hbm, mv, load_sem.at[1]),
        pltpu.make_async_copy(q_hbm, qv, load_sem.at[2]),
    ]

    barrier = pltpu.get_barrier_semaphore()
    for name, index, size in (("dp", d, n), ("layer", l, layers), ("query", q, queries)):
        for step in range(1, size):
            pl.semaphore_signal(
                barrier, inc=1, device_id={name: other(index, step, size)}, device_id_type=MESH
            )
    for load in loads:
        load.start()
    pl.semaphore_wait(barrier, n + layers + queries - 3)

    cols = pl.ds(pl.multiple_of(q * col_width, LANES), col_width)
    own_in_col = pl.ds(offset, own_width)

    def z_copy(way, step, c, first):
        block = d - step if way == 0 else d + step
        at = pl.ds(c * piece, piece)
        src = m_hbm.at[at, cols] if first else gcol.at[block, at]
        return remote(
            src, gcol.at[block, at], z_send.at[way, step, c], z_recv.at[way, step, c],
            dp=d + 1 if way == 0 else d - 1,
        )

    def sends(way, step):
        if way == 0:
            return jnp.logical_and(d < n - 1, d - step >= 0)
        return jnp.logical_and(d > 0, d + step <= n - 1)

    def arrives(way, step):
        if way == 0:
            return d - 1 - step >= 0
        return d + 1 + step <= n - 1

    def incoming(way, step):
        return d - 1 - step if way == 0 else d + 1 + step

    for c in range(pieces):
        for way in (0, 1):
            @pl.when(sends(way, 0))
            def _(way=way, c=c):
                z_copy(way, 0, c, True).start()

    e_rows = pl.ds(pl.multiple_of(q * col_blocks, 8), col_blocks)

    def e_copy(step):
        return remote(
            e_hbm.at[e_rows], ecol.at[d], e_send.at[step - 1], e_recv.at[step - 1],
            dp=other(d, step, n),
        )

    for step in range(1, n):
        e_copy(step).start()

    for load in loads:
        load.wait()
    scales = scale_columns(ev[...])
    for j in range(width // LANES):
        at = slice(j * LANES, (j + 1) * LANES)
        mv[:, at] = mv[:, at] * spread(scales[:, j:j + 1])
    scores = jnp.zeros((rows, qv.shape[0]), jnp.float32)
    depth = width // 4
    for j in range(4):
        at = slice(j * depth, (j + 1) * depth)
        scores += lax.dot_general(
            mv[:, at], qv[:, at], (((1,), (1,)), ((), ())), preferred_element_type=jnp.float32
        )
    docs = owner_ref.shape[1]
    slot_of = (
        lax.broadcasted_iota(jnp.int32, (docs, docs), 0) == owner_ref[...]
    ).astype(jnp.float32).astype(jnp.bfloat16)
    doc_of = (
        lax.broadcasted_iota(jnp.int32, (docs, rows), 0) == doc_ref[...]
    ).astype(jnp.float32).astype(jnp.bfloat16)
    member = jnp.dot(slot_of, doc_of, preferred_element_type=jnp.float32).astype(jnp.bfloat16)
    high = scores.astype(jnp.bfloat16)
    rest = scores - high.astype(jnp.float32)
    middle = rest.astype(jnp.bfloat16)
    low = (rest - middle.astype(jnp.float32)).astype(jnp.bfloat16)
    summed = (
        jnp.dot(member, low, preferred_element_type=jnp.float32)
        + jnp.dot(member, middle, preferred_element_type=jnp.float32)
    ) + jnp.dot(member, high, preferred_element_type=jnp.float32)
    terms[...] = summed.reshape(terms.shape)

    def x_copy(step):
        to = other(l, step, layers)
        return remote(
            terms.at[:, to], from_layers.at[step - 1],
            x_send.at[step - 1], x_recv.at[step - 1], layer=to,
        )

    def s_copy(step):
        to = other(d, step, n)
        return remote(
            part.at[to], from_dp.at[step - 1], s_send.at[step - 1], s_recv.at[step - 1], dp=to
        )

    def r_copy(step):
        to = other(l, step, layers)
        return remote(
            total.at[l], total.at[l], r_send.at[step - 1], r_recv.at[step - 1], layer=to
        )

    for step in range(1, layers):
        x_copy(step).start()

    def over_layers():
        for step in range(1, layers):
            x_copy(step).wait_recv()
        value = terms[:, l]
        for step in range(1, layers):
            value = value + from_layers[step - 1]
        part[...] = value
        for step in range(1, n):
            s_copy(step).start()

    def over_dp():
        for step in range(1, n):
            s_copy(step).wait_recv()
        value = part[d]
        for step in range(1, n):
            value = value + from_dp[step - 1]
        total[l] = value
        for step in range(1, layers):
            r_copy(step).start()

    def f_copy(step, to_step):
        block = other(d, -step, n)
        return remote(
            ecol.at[block], eown.at[block], f_send.at[step - 1, to_step - 1], f_recv.at[step - 1],
            query=other(q, to_step, queries),
        )

    def exponents_on():
        for step in range(1, n):
            e_copy(step).wait_recv()

        @pl.when(q == source)
        def _():
            for step in range(1, n):
                for to_step in range(1, queries):
                    f_copy(step, to_step).start()

    core = lax.rem(q, 2)
    source_core = lax.rem(source, 2)
    sibling = q + 1 - 2 * core
    is_source = q == source
    is_relay = jnp.logical_and(q != source, core == source_core)

    def o_copy(way, step, c, k, from_source):
        block = incoming(way, step)
        at = pl.ds(c * piece, piece)
        src = gcol.at[block, at, own_in_col] if from_source else gown.at[block, at]
        to = sibling if k == 0 else other(q, 2 * k, queries)
        return remote(
            src, gown.at[block, at], o_send.at[way, step, c, k], o_recv.at[way, step, c], query=to
        )

    def on_arrival(way, step, c):
        @pl.when(arrives(way, step))
        def _():
            z_copy(way, step, c, False).wait_recv()

            @pl.when(sends(way, step + 1))
            def _():
                z_copy(way, step + 1, c, False).start()

            @pl.when(is_source)
            def _():
                for k in reversed(range(queries // 2)):
                    o_copy(way, step, c, k, True).start()

    def on_own(way, step, c):
        @pl.when(jnp.logical_and(arrives(way, step), q != source))
        def _():
            o_copy(way, step, c, 0, False).wait_recv()

            @pl.when(is_relay)
            def _():
                o_copy(way, step, c, 0, False).start()

    items = [(way, step, c) for step in range(n - 1) for c in range(pieces) for way in (0, 1)]
    lag = 4
    for i in range(len(items) + lag):
        if i < len(items):
            on_arrival(*items[i])
        if i >= lag:
            on_own(*items[i - lag])
        if i == 1:
            over_layers()
        if i == 3:
            exponents_on()
        if i == 5:
            over_dp()

    for step in range(1, layers):
        r_copy(step).wait_recv()
    out = pltpu.make_async_copy(total, ds_out, out_sem)
    out.start()

    @pl.when(q != source)
    def _():
        for step in range(1, n):
            f_copy(step, 1).wait_recv()

    @pl.when(q == source)
    def _():
        for step in range(1, n):
            for to_step in range(1, queries):
                f_copy(step, to_step).wait_send()

    for step in range(1, n):
        e_copy(step).wait_send()
        s_copy(step).wait_send()
    for step in range(1, layers):
        x_copy(step).wait_send()
        r_copy(step).wait_send()
    for way, step, c in items:
        @pl.when(sends(way, step))
        def _(way=way, step=step, c=c):
            z_copy(way, step, c, step == 0).wait_send()

        @pl.when(jnp.logical_and(arrives(way, step), is_source))
        def _(way=way, step=step, c=c):
            for k in range(queries // 2):
                o_copy(way, step, c, k, True).wait_send()

        @pl.when(jnp.logical_and(arrives(way, step), is_relay))
        def _(way=way, step=step, c=c):
            o_copy(way, step, c, 0, False).wait_send()
    out.wait()


def fisher_kernel(
    sizes, m_hbm, e_hbm, gcol, gown, ecol, eown, ds_in, fisher, ds_out,
    cv, ov, ecv, eov, tile, dsv, c_sem, o_sem, ec_sem, eo_sem, t_sem, ds_sem,
):
    n, queries, own_width = sizes
    rows, width = m_hbm.shape
    col_width = width // queries
    col_blocks, own_blocks = col_width // LANES, own_width // LANES
    d, q = lax.axis_index("dp"), lax.axis_index("query")
    source = lax.div(d * own_width, col_width)
    offset = pl.multiple_of(lax.rem(d * own_width, col_width), LANES)
    cols = pl.ds(pl.multiple_of(q * col_width, LANES), col_width)
    owns = pl.ds(pl.multiple_of(d * own_width, LANES), own_width)
    ds_load = pltpu.make_async_copy(ds_in, dsv, ds_sem.at[0])
    ds_store = pltpu.make_async_copy(dsv, ds_out, ds_sem.at[1])

    def c_copy(src, b):
        return pltpu.make_async_copy(src, cv.at[pl.ds(b * rows, rows)], c_sem.at[b])

    def o_copy(src, b):
        return pltpu.make_async_copy(src, ov.at[pl.ds(b * rows, rows)], o_sem.at[b])

    def e_rows(index):
        return e_hbm.at[pl.ds(pl.multiple_of(index * col_blocks, 8), col_blocks)]

    for b in range(n):
        @pl.when(b == d)
        def _(b=b):
            pltpu.make_async_copy(e_rows(q), ecv.at[b], ec_sem.at[b]).start()
            pltpu.make_async_copy(e_rows(source), eov.at[b], eo_sem.at[b]).start()
            c_copy(m_hbm.at[:, cols], b).start()
            o_copy(m_hbm.at[:, owns], b).start()

        @pl.when(b != d)
        def _(b=b):
            pltpu.make_async_copy(ecol.at[b], ecv.at[b], ec_sem.at[b]).start()
            c_copy(gcol.at[b], b).start()

            @pl.when(q == source)
            def _():
                pltpu.make_async_copy(ecol.at[b], eov.at[b], eo_sem.at[b]).start()
                o_copy(gcol.at[b, :, pl.ds(offset, own_width)], b).start()

            @pl.when(q != source)
            def _():
                pltpu.make_async_copy(eown.at[b], eov.at[b], eo_sem.at[b]).start()
                o_copy(gown.at[b], b).start()
    ds_load.start()

    lane = lax.broadcasted_iota(jnp.int32, (rows, col_blocks), 1)
    for b in range(n):
        at_rows = slice(b * rows, (b + 1) * rows)
        pltpu.make_async_copy(ecol.at[b], ecv.at[b], ec_sem.at[b]).wait()
        c_copy(gcol.at[b], b).wait()
        scales = scale_columns(ecv[b])
        for j in range(col_blocks):
            at = slice(j * LANES, (j + 1) * LANES)
            cv[at_rows, at] = cv[at_rows, at] * spread(scales[:, j:j + 1])
        pltpu.make_async_copy(eown.at[b], eov.at[b], eo_sem.at[b]).wait()
        o_copy(gown.at[b], b).wait()
        scales = scale_columns(eov[b])
        for j in range(own_blocks):
            if own_blocks == col_blocks:
                scale = scales[:, j:j + 1]
            else:
                chosen = lane == lax.div(offset, LANES) + j
                scale = jnp.sum(jnp.where(chosen, scales, 0.0), axis=1, keepdims=True)
            at = slice(j * LANES, (j + 1) * LANES)
            ov[at_rows, at] = ov[at_rows, at] * spread(scale)

    ds_load.wait()
    ds_store.start()
    height = tile.shape[1]
    steps = own_width // height

    def t_copy(i):
        return pltpu.make_async_copy(
            tile.at[i], fisher.at[0, pl.ds(pl.multiple_of(i * height, 8), height)], t_sem.at[i]
        )

    def body(i, _):
        at = pl.ds(pl.multiple_of(i * height, LANES), height)
        block = lax.dot_general(
            ov[:, at], cv[...], (((0,), (0,)), ((), ())), preferred_element_type=jnp.float32
        )
        tile[i] = block * (1.0 / (n * rows))
        t_copy(i).start()
        return 0

    lax.fori_loop(0, steps, body, 0)
    for i in range(steps):
        t_copy(i).wait()
    ds_store.wait()


def per_device(mantissas, exponents, queries, doc_ids, owners):
    n, layers, nq = (lax.axis_size(a) for a in ("dp", "layer", "query"))
    rows, _, width = mantissas.shape
    m = mantissas.reshape(rows, width)
    e = jnp.transpose(exponents[:, 0, :])
    qs = queries.reshape(queries.shape[0], width)
    docs = owners.shape[0]
    own_width, col_width = width // n, width // nq
    col_blocks = col_width // LANES
    slots = docs // n
    sub = slots // layers
    pieces = max(1, 16 // n)
    count = qs.shape[0]
    f32, bf16 = jnp.float32, jnp.bfloat16
    dma = pltpu.SemaphoreType.DMA
    anyspace = pl.BlockSpec(memory_space=pl.ANY)
    vmem = pl.BlockSpec(memory_space=pltpu.VMEM)
    gcol, gown, ecol, eown, ds = pl.pallas_call(
        functools.partial(gather_kernel, (n, layers, nq, pieces, own_width)),
        out_shape=(
            jax.ShapeDtypeStruct((n, rows, col_width), bf16),
            jax.ShapeDtypeStruct((n, rows, own_width), bf16),
            jax.ShapeDtypeStruct((n, col_blocks, rows), jnp.int32),
            jax.ShapeDtypeStruct((n, col_blocks, rows), jnp.int32),
            jax.ShapeDtypeStruct((layers, sub, count), f32),
        ),
        in_specs=[anyspace, anyspace, anyspace, vmem, vmem],
        out_specs=(anyspace,) * 5,
        scratch_shapes=[
            pltpu.VMEM((rows, width), bf16),
            pltpu.VMEM((count, width), bf16),
            pltpu.VMEM(e.shape, jnp.int32),
            pltpu.VMEM((n, layers, sub, count), f32),
            pltpu.VMEM((layers - 1, n, sub, count), f32),
            pltpu.VMEM((n, sub, count), f32),
            pltpu.VMEM((n - 1, sub, count), f32),
            pltpu.VMEM((layers, sub, count), f32),
            dma((3,)),
            dma((2, n - 1, pieces)),
            dma((2, n - 1, pieces)),
            dma((2, n - 1, pieces, nq // 2)),
            dma((2, n - 1, pieces)),
            dma((n - 1,)),
            dma((n - 1,)),
            dma((n - 1, nq - 1)),
            dma((n - 1,)),
            dma((layers - 1,)),
            dma((layers - 1,)),
            dma((n - 1,)),
            dma((n - 1,)),
            dma((layers - 1,)),
            dma((layers - 1,)),
            dma,
        ],
        compiler_params=pltpu.CompilerParams(
            collective_id=0, has_side_effects=True, vmem_limit_bytes=32 * 2**20
        ),
        name="gather",
    )(m, e, qs, doc_ids.reshape(1, rows), owners.reshape(1, docs))
    height = min(256, own_width)
    steps = own_width // height
    fisher, ds = pl.pallas_call(
        functools.partial(fisher_kernel, (n, nq, own_width)),
        out_shape=(
            jax.ShapeDtypeStruct((1, own_width, col_width), f32),
            jax.ShapeDtypeStruct((layers, sub, count), f32),
        ),
        in_specs=[anyspace] * 7,
        out_specs=(anyspace, anyspace),
        scratch_shapes=[
            pltpu.VMEM((n * rows, col_width), bf16),
            pltpu.VMEM((n * rows, own_width), bf16),
            pltpu.VMEM((n, col_blocks, rows), jnp.int32),
            pltpu.VMEM((n, col_blocks, rows), jnp.int32),
            pltpu.VMEM((steps, height, col_width), f32),
            pltpu.VMEM((layers, sub, count), f32),
            dma((n,)),
            dma((n,)),
            dma((n,)),
            dma((n,)),
            dma((steps,)),
            dma((2,)),
        ],
        compiler_params=pltpu.CompilerParams(vmem_limit_bytes=48 * 2**20),
        name="fisher",
    )(m, e, gcol, gown, ecol, eown, ds)
    return fisher, ds.reshape(slots, count)


def solution(mesh):
    in_specs = (
        P("dp", "layer", None),
        P("dp", "layer", None),
        P("query", "layer", None),
        P("dp"),
        P(),
    )
    out_specs = (P("layer", "dp", "query"), P("dp", "query"))
    return jax.shard_map(
        per_device, mesh=mesh, in_specs=in_specs, out_specs=out_specs, check_vma=False
    )
```

```python
import functools

import jax
import jax.numpy as jnp
from jax import lax
from jax.experimental import pallas as pl
from jax.experimental.pallas import tpu as pltpu
from jax.sharding import PartitionSpec as P

MESH = pl.DeviceIdType.MESH
LANES = 128


def remote(src, dst, send, recv, **target):
    return pltpu.make_async_remote_copy(
        src_ref=src, dst_ref=dst, send_sem=send, recv_sem=recv,
        device_id=target, device_id_type=MESH,
    )


def scale_columns(exps):
    return jnp.transpose(jnp.exp2(exps.astype(jnp.float32)))


def spread(scale, width=LANES):
    return jnp.broadcast_to(scale, (scale.shape[0], width)).astype(jnp.bfloat16)


def gather_kernel(
    sizes, m_hbm, e_hbm, q_hbm, doc_hbm, owner_hbm,
    acc_out, col_out, own_out, ds_out,
    gcol, gown, ecol, eown, dcol, down, acc,
    mv, qv, ev, doc_ref, owner_ref, terms, from_layers, part, from_dp, total,
    load_sem, l_sem, z_send, z_recv, o_send, o_recv, e_send, e_recv, f_send, f_recv,
    x_send, x_recv, s_send, s_recv, r_send, r_recv, out_sem,
):
    n, layers, queries, pieces, own_width = sizes
    rows, width = m_hbm.shape
    col_width = width // queries
    col_blocks = col_width // LANES
    piece = rows // pieces
    d, l, q = (lax.axis_index(a) for a in ("dp", "layer", "query"))
    source = lax.div(d * own_width, col_width)
    offset = pl.multiple_of(lax.rem(d * own_width, col_width), LANES)
    sub = terms.shape[2]

    def other(index, step, size):
        return lax.rem(index + step + size, size)

    loads = [
        pltpu.make_async_copy(e_hbm, ev, load_sem.at[0]),
        pltpu.make_async_copy(m_hbm, mv, load_sem.at[1]),
        pltpu.make_async_copy(q_hbm, qv, load_sem.at[2]),
        pltpu.make_async_copy(doc_hbm, doc_ref, load_sem.at[3]),
        pltpu.make_async_copy(owner_hbm, owner_ref, load_sem.at[4]),
    ]

    barrier = pltpu.get_barrier_semaphore()
    for name, index, size in (("dp", d, n), ("layer", l, layers), ("query", q, queries)):
        for step in range(1, size):
            pl.semaphore_signal(
                barrier, inc=1, device_id={name: other(index, step, size)}, device_id_type=MESH
            )
    for load in loads:
        load.start()
    pl.semaphore_wait(barrier, n + layers + queries - 3)

    cols = pl.ds(pl.multiple_of(q * col_width, LANES), col_width)
    own_in_col = pl.ds(offset, own_width)

    def z_copy(way, step, c, first):
        block = d - step if way == 0 else d + step
        at = pl.ds(c * piece, piece)
        src = m_hbm.at[at, cols] if first else gcol.at[block, at]
        return remote(
            src, gcol.at[block, at], z_send.at[way, step, c], z_recv.at[way, step, c],
            dp=d + 1 if way == 0 else d - 1,
        )

    def sends(way, step):
        if way == 0:
            return jnp.logical_and(d < n - 1, d - step >= 0)
        return jnp.logical_and(d > 0, d + step <= n - 1)

    def arrives(way, step):
        if way == 0:
            return d - 1 - step >= 0
        return d + 1 + step <= n - 1

    def incoming(way, step):
        return d - 1 - step if way == 0 else d + 1 + step

    for c in range(pieces):
        for way in (0, 1):
            @pl.when(sends(way, 0))
            def _(way=way, c=c):
                z_copy(way, 0, c, True).start()

    e_rows = pl.ds(pl.multiple_of(q * col_blocks, 8), col_blocks)

    def e_copy(step):
        return remote(
            e_hbm.at[e_rows], ecol.at[d], e_send.at[step - 1], e_recv.at[step - 1],
            dp=other(d, step, n),
        )

    for step in range(1, n):
        e_copy(step).start()

    for load in loads:
        load.wait()
    scales = scale_columns(ev[...])
    for j in range(width // LANES):
        at = slice(j * LANES, (j + 1) * LANES)
        mv[:, at] = mv[:, at] * spread(scales[:, j:j + 1])
    scores = jnp.zeros((rows, qv.shape[0]), jnp.float32)
    depth = width // 4
    for j in range(4):
        at = slice(j * depth, (j + 1) * depth)
        scores += lax.dot_general(
            mv[:, at], qv[:, at], (((1,), (1,)), ((), ())), preferred_element_type=jnp.float32
        )
    docs = owner_ref.shape[1]
    slot_of = (
        lax.broadcasted_iota(jnp.int32, (docs, docs), 0) == owner_ref[...]
    ).astype(jnp.float32).astype(jnp.bfloat16)
    doc_of = (
        lax.broadcasted_iota(jnp.int32, (docs, rows), 0) == doc_ref[...]
    ).astype(jnp.float32).astype(jnp.bfloat16)
    member = jnp.dot(slot_of, doc_of, preferred_element_type=jnp.float32).astype(jnp.bfloat16)
    high = scores.astype(jnp.bfloat16)
    rest = scores - high.astype(jnp.float32)
    middle = rest.astype(jnp.bfloat16)
    low = (rest - middle.astype(jnp.float32)).astype(jnp.bfloat16)
    summed = (
        jnp.dot(member, low, preferred_element_type=jnp.float32)
        + jnp.dot(member, middle, preferred_element_type=jnp.float32)
    ) + jnp.dot(member, high, preferred_element_type=jnp.float32)
    terms[...] = summed.reshape(terms.shape)

    def x_copy(step):
        to = other(l, step, layers)
        return remote(
            terms.at[:, to], from_layers.at[step - 1],
            x_send.at[step - 1], x_recv.at[step - 1], layer=to,
        )

    def s_copy(step):
        to = other(d, step, n)
        return remote(
            part.at[to], from_dp.at[step - 1], s_send.at[step - 1], s_recv.at[step - 1], dp=to
        )

    def r_copy(step):
        to = other(l, step, layers)
        return remote(
            total.at[l], total.at[l], r_send.at[step - 1], r_recv.at[step - 1], layer=to
        )

    for step in range(1, layers):
        x_copy(step).start()

    height = min(256, own_width)

    def add_block(own_of, col, first):
        def body(i, _):
            at = pl.ds(pl.multiple_of(i * height, LANES), height)
            block = lax.dot_general(
                own_of(i * height), col[...], (((0,), (0,)), ((), ())),
                preferred_element_type=jnp.float32,
            )
            acc[at] = block if first else acc[at] + block
            return 0

        lax.fori_loop(0, own_width // height, body, 0)

    add_block(
        lambda start: mv[:, pl.ds(pl.multiple_of(d * own_width + start, LANES), height)],
        mv.at[:, cols], True,
    )

    def over_layers():
        for step in range(1, layers):
            x_copy(step).wait_recv()
        value = terms[:, l]
        for step in range(1, layers):
            value = value + from_layers[step - 1]
        part[...] = value
        for step in range(1, n):
            s_copy(step).start()

    def over_dp():
        for step in range(1, n):
            s_copy(step).wait_recv()
        value = part[d]
        for step in range(1, n):
            value = value + from_dp[step - 1]
        total[l] = value
        for step in range(1, layers):
            r_copy(step).start()

    def f_copy(step, to_step):
        block = other(d, -step, n)
        return remote(
            ecol.at[block], eown.at[block], f_send.at[step - 1, to_step - 1], f_recv.at[step - 1],
            query=other(q, to_step, queries),
        )

    def exponents_on():
        for step in range(1, n):
            e_copy(step).wait_recv()

        @pl.when(q == source)
        def _():
            for step in range(1, n):
                for to_step in range(1, queries):
                    f_copy(step, to_step).start()

        @pl.when(q != source)
        def _():
            for step in range(1, n):
                f_copy(step, 1).wait_recv()

    core = lax.rem(q, 2)
    source_core = lax.rem(source, 2)
    sibling = q + 1 - 2 * core
    is_source = q == source
    is_relay = jnp.logical_and(q != source, core == source_core)

    def o_copy(way, step, c, k, from_source):
        block = incoming(way, step)
        at = pl.ds(c * piece, piece)
        src = gcol.at[block, at, own_in_col] if from_source else gown.at[block, at]
        to = sibling if k == 0 else other(q, 2 * k, queries)
        return remote(
            src, gown.at[block, at], o_send.at[way, step, c, k], o_recv.at[way, step, c], query=to
        )

    def on_arrival(way, step, c):
        @pl.when(arrives(way, step))
        def _():
            z_copy(way, step, c, False).wait_recv()

            @pl.when(sends(way, step + 1))
            def _():
                z_copy(way, step + 1, c, False).start()

            @pl.when(is_source)
            def _():
                for k in reversed(range(queries // 2)):
                    o_copy(way, step, c, k, True).start()

    last = jnp.where(d >= (n + 1) // 2, 0, n - 1)
    own_blocks = own_width // LANES
    acc_copy = pltpu.make_async_copy(acc, acc_out, l_sem.at[0, 0])

    def last_copies(way, c):
        at = pl.ds(c * piece, piece)
        return (
            pltpu.make_async_copy(dcol.at[way, at], col_out.at[at], l_sem.at[1, c]),
            pltpu.make_async_copy(down.at[way, at], own_out.at[at], l_sem.at[2, c]),
        )

    def on_own(way, step, c):
        @pl.when(arrives(way, step))
        def _():
            block = incoming(way, step)
            at = pl.ds(c * piece, piece)
            here = slice(c * piece, (c + 1) * piece)
            scales = scale_columns(ecol[block])[here]
            for j in range(col_blocks):
                lanes = slice(j * LANES, (j + 1) * LANES)
                dcol[way, at, lanes] = gcol[block, at, lanes] * spread(scales[:, j:j + 1])

            def own_piece(source_ref, base):
                scales = scale_columns(
                    ecol[block] if source_ref is gcol else eown[block]
                )[here]
                lane = lax.broadcasted_iota(jnp.int32, scales.shape, 1)
                for j in range(own_blocks):
                    if own_blocks == col_blocks:
                        scale = scales[:, j:j + 1]
                    else:
                        chosen = lane == lax.div(offset, LANES) + j
                        scale = jnp.sum(jnp.where(chosen, scales, 0.0), axis=1, keepdims=True)
                    from_lanes = pl.ds(pl.multiple_of(base + j * LANES, LANES), LANES)
                    down[way, at, j * LANES:(j + 1) * LANES] = (
                        source_ref[block, at, from_lanes] * spread(scale)
                    )

            @pl.when(q == source)
            def _():
                own_piece(gcol, offset)

            @pl.when(q != source)
            def _():
                o_copy(way, step, c, 0, False).wait_recv()

                @pl.when(is_relay)
                def _():
                    o_copy(way, step, c, 0, False).start()

                own_piece(gown, 0)

            @pl.when(block == last)
            def _():
                for copy in last_copies(way, c):
                    copy.start()

            if c == pieces - 1:
                @pl.when(block != last)
                def _():
                    add_block(
                        lambda start: down[way, :, pl.ds(pl.multiple_of(start, LANES), height)],
                        dcol.at[way], False,
                    )

    items = [(way, step, c) for step in range(n - 1) for c in range(pieces) for way in (0, 1)]
    lag = 4
    for i in range(len(items) + lag):
        if i < len(items):
            on_arrival(*items[i])
        if i >= lag:
            on_own(*items[i - lag])
        if i == 1:
            over_layers()
        if i == 3:
            exponents_on()
        if i == 5:
            over_dp()

    acc_copy.start()
    for step in range(1, layers):
        r_copy(step).wait_recv()
    out = pltpu.make_async_copy(total, ds_out, out_sem)
    out.start()

    @pl.when(q == source)
    def _():
        for step in range(1, n):
            for to_step in range(1, queries):
                f_copy(step, to_step).wait_send()

    for step in range(1, n):
        e_copy(step).wait_send()
        s_copy(step).wait_send()
    for step in range(1, layers):
        x_copy(step).wait_send()
        r_copy(step).wait_send()
    for way, step, c in items:
        @pl.when(sends(way, step))
        def _(way=way, step=step, c=c):
            z_copy(way, step, c, step == 0).wait_send()

        @pl.when(jnp.logical_and(arrives(way, step), is_source))
        def _(way=way, step=step, c=c):
            for k in range(queries // 2):
                o_copy(way, step, c, k, True).wait_send()

        @pl.when(jnp.logical_and(arrives(way, step), is_relay))
        def _(way=way, step=step, c=c):
            o_copy(way, step, c, 0, False).wait_send()
    for c in range(pieces):
        for copy in last_copies(0, c):
            copy.wait()
    acc_copy.wait()
    out.wait()


def fisher_kernel(scale, acc, col, own, ds_in, fisher, ds_out, tile, t_sem, ds_sem):
    ds_copy = pltpu.make_async_copy(ds_in, ds_out, ds_sem)
    ds_copy.start()
    steps, height, _ = tile.shape

    def t_copy(i):
        return pltpu.make_async_copy(
            tile.at[i], fisher.at[0, pl.ds(pl.multiple_of(i * height, 8), height)], t_sem.at[i]
        )

    def body(i, _):
        at = pl.ds(pl.multiple_of(i * height, LANES), height)
        block = lax.dot_general(
            own[:, at], col[...], (((0,), (0,)), ((), ())), preferred_element_type=jnp.float32
        )
        tile[i] = (acc[at] + block) * scale
        t_copy(i).start()
        return 0

    lax.fori_loop(0, steps, body, 0)
    for i in range(steps):
        t_copy(i).wait()
    ds_copy.wait()


def per_device(mantissas, exponents, queries, doc_ids, owners):
    n, layers, nq = (lax.axis_size(a) for a in ("dp", "layer", "query"))
    rows, _, width = mantissas.shape
    m = mantissas.reshape(rows, width)
    e = jnp.transpose(exponents[:, 0, :])
    qs = queries.reshape(queries.shape[0], width)
    docs = owners.shape[0]
    own_width, col_width = width // n, width // nq
    col_blocks = col_width // LANES
    slots = docs // n
    sub = slots // layers
    pieces = max(1, 16 // n)
    count = qs.shape[0]
    f32, bf16 = jnp.float32, jnp.bfloat16
    dma = pltpu.SemaphoreType.DMA
    anyspace = pl.BlockSpec(memory_space=pl.ANY)
    vmem = pl.BlockSpec(memory_space=pltpu.VMEM)
    hbm = pl.BlockSpec(memory_space=pltpu.HBM)
    acc, col, own, ds = pl.pallas_call(
        functools.partial(gather_kernel, (n, layers, nq, pieces, own_width)),
        out_shape=(
            pltpu.VMEM((own_width, col_width), f32),
            pltpu.VMEM((rows, col_width), bf16),
            pltpu.VMEM((rows, own_width), bf16),
            pltpu.VMEM((layers, sub, count), f32),
        ),
        in_specs=[hbm] * 5,
        out_specs=(anyspace,) * 4,
        scratch_shapes=[
            pltpu.VMEM((n, rows, col_width), bf16),
            pltpu.VMEM((n, rows, own_width), bf16),
            pltpu.VMEM((n, col_blocks, rows), jnp.int32),
            pltpu.VMEM((n, col_blocks, rows), jnp.int32),
            pltpu.VMEM((2, rows, col_width), bf16),
            pltpu.VMEM((2, rows, own_width), bf16),
            pltpu.VMEM((own_width, col_width), f32),
            pltpu.VMEM((rows, width), bf16),
            pltpu.VMEM((count, width), bf16),
            pltpu.VMEM(e.shape, jnp.int32),
            pltpu.VMEM((1, rows), jnp.int32),
            pltpu.VMEM((1, docs), jnp.int32),
            pltpu.VMEM((n, layers, sub, count), f32),
            pltpu.VMEM((layers - 1, n, sub, count), f32),
            pltpu.VMEM((n, sub, count), f32),
            pltpu.VMEM((n - 1, sub, count), f32),
            pltpu.VMEM((layers, sub, count), f32),
            dma((5,)),
            dma((3, pieces)),
            dma((2, n - 1, pieces)),
            dma((2, n - 1, pieces)),
            dma((2, n - 1, pieces, nq // 2)),
            dma((2, n - 1, pieces)),
            dma((n - 1,)),
            dma((n - 1,)),
            dma((n - 1, nq - 1)),
            dma((n - 1,)),
            dma((layers - 1,)),
            dma((layers - 1,)),
            dma((n - 1,)),
            dma((n - 1,)),
            dma((layers - 1,)),
            dma((layers - 1,)),
            dma,
        ],
        compiler_params=pltpu.CompilerParams(
            collective_id=0, has_side_effects=True, vmem_limit_bytes=58 * 2**20
        ),
        name="gather",
    )(m, e, qs, doc_ids.reshape(1, rows), owners.reshape(1, docs))
    height = min(128, own_width)
    steps = own_width // height
    fisher, ds = pl.pallas_call(
        functools.partial(fisher_kernel, 1.0 / (n * rows)),
        out_shape=(
            jax.ShapeDtypeStruct((1, own_width, col_width), f32),
            jax.ShapeDtypeStruct((layers, sub, count), f32),
        ),
        in_specs=[vmem] * 4,
        out_specs=(hbm, hbm),
        scratch_shapes=[
            pltpu.VMEM((steps, height, col_width), f32),
            dma((steps,)),
            dma,
        ],
        compiler_params=pltpu.CompilerParams(vmem_limit_bytes=16 * 2**20),
        name="fisher",
    )(acc, col, own, ds)
    return fisher, ds.reshape(slots, count)


def solution(mesh):
    in_specs = (
        P("dp", "layer", None),
        P("dp", "layer", None),
        P("query", "layer", None),
        P("dp"),
        P(),
    )
    out_specs = (P("layer", "dp", "query"), P("dp", "query"))
    return jax.shard_map(
        per_device, mesh=mesh, in_specs=in_specs, out_specs=out_specs, check_vma=False
    )
```

```python
import functools

import jax
import jax.numpy as jnp
from jax import lax
from jax.experimental import pallas as pl
from jax.experimental.pallas import tpu as pltpu
from jax.sharding import PartitionSpec as P

MESH = pl.DeviceIdType.MESH
LANES = 128


def remote(src, dst, send, recv, **target):
    return pltpu.make_async_remote_copy(
        src_ref=src, dst_ref=dst, send_sem=send, recv_sem=recv,
        device_id=target, device_id_type=MESH,
    )


def scale_columns(exps):
    return jnp.transpose(jnp.exp2(exps.astype(jnp.float32)))


def spread(scale, width=LANES):
    return jnp.broadcast_to(scale, (scale.shape[0], width)).astype(jnp.bfloat16)


def gather_kernel(
    sizes, m_hbm, e_hbm, q_hbm, doc_hbm, owner_hbm,
    acc, col_out, own_out, ds_out,
    gcol, gown, ecol, eown, dcol, down,
    mv, qv, ev, doc_ref, owner_ref, terms, from_layers, part, from_dp, total,
    load_sem, z_send, z_recv, o_send, o_recv, e_send, e_recv, f_send, f_recv,
    x_send, x_recv, s_send, s_recv, r_send, r_recv,
):
    n, layers, queries, pieces, own_width = sizes
    rows, width = m_hbm.shape
    col_width = width // queries
    col_blocks = col_width // LANES
    piece = rows // pieces
    d, l, q = (lax.axis_index(a) for a in ("dp", "layer", "query"))
    source = lax.div(d * own_width, col_width)
    offset = pl.multiple_of(lax.rem(d * own_width, col_width), LANES)
    sub = terms.shape[2]

    def other(index, step, size):
        return lax.rem(index + step + size, size)

    loads = [
        pltpu.make_async_copy(e_hbm, ev, load_sem.at[0]),
        pltpu.make_async_copy(m_hbm, mv, load_sem.at[1]),
        pltpu.make_async_copy(q_hbm, qv, load_sem.at[2]),
        pltpu.make_async_copy(doc_hbm, doc_ref, load_sem.at[3]),
        pltpu.make_async_copy(owner_hbm, owner_ref, load_sem.at[4]),
    ]

    barrier = pltpu.get_barrier_semaphore()
    for name, index, size in (("dp", d, n), ("layer", l, layers), ("query", q, queries)):
        for step in range(1, size):
            pl.semaphore_signal(
                barrier, inc=1, device_id={name: other(index, step, size)}, device_id_type=MESH
            )
    for load in loads:
        load.start()
    pl.semaphore_wait(barrier, n + layers + queries - 3)

    cols = pl.ds(pl.multiple_of(q * col_width, LANES), col_width)
    own_in_col = pl.ds(offset, own_width)

    def z_copy(way, step, c, first):
        block = d - step if way == 0 else d + step
        at = pl.ds(c * piece, piece)
        src = m_hbm.at[at, cols] if first else gcol.at[block, at]
        return remote(
            src, gcol.at[block, at], z_send.at[way, step, c], z_recv.at[way, step, c],
            dp=d + 1 if way == 0 else d - 1,
        )

    def sends(way, step):
        if way == 0:
            return jnp.logical_and(d < n - 1, d - step >= 0)
        return jnp.logical_and(d > 0, d + step <= n - 1)

    def arrives(way, step):
        if way == 0:
            return d - 1 - step >= 0
        return d + 1 + step <= n - 1

    def incoming(way, step):
        return d - 1 - step if way == 0 else d + 1 + step

    e_rows = pl.ds(pl.multiple_of(q * col_blocks, 8), col_blocks)

    def e_copy(step):
        return remote(
            e_hbm.at[e_rows], ecol.at[d], e_send.at[step - 1], e_recv.at[step - 1],
            dp=other(d, step, n),
        )

    for step in range(1, n):
        e_copy(step).start()

    for c in range(pieces):
        for way in (0, 1):
            @pl.when(sends(way, 0))
            def _(way=way, c=c):
                z_copy(way, 0, c, True).start()

    for load in loads:
        load.wait()
    scales = scale_columns(ev[...])
    for j in range(width // LANES):
        at = slice(j * LANES, (j + 1) * LANES)
        mv[:, at] = mv[:, at] * spread(scales[:, j:j + 1])
    scores = jnp.zeros((rows, qv.shape[0]), jnp.float32)
    depth = width // 4
    for j in range(4):
        at = slice(j * depth, (j + 1) * depth)
        scores += lax.dot_general(
            mv[:, at], qv[:, at], (((1,), (1,)), ((), ())), preferred_element_type=jnp.float32
        )
    docs = owner_ref.shape[1]
    slot_of = (
        lax.broadcasted_iota(jnp.int32, (docs, docs), 0) == owner_ref[...]
    ).astype(jnp.float32).astype(jnp.bfloat16)
    doc_of = (
        lax.broadcasted_iota(jnp.int32, (docs, rows), 0) == doc_ref[...]
    ).astype(jnp.float32).astype(jnp.bfloat16)
    member = jnp.dot(slot_of, doc_of, preferred_element_type=jnp.float32).astype(jnp.bfloat16)
    high = scores.astype(jnp.bfloat16)
    rest = scores - high.astype(jnp.float32)
    middle = rest.astype(jnp.bfloat16)
    low = (rest - middle.astype(jnp.float32)).astype(jnp.bfloat16)
    summed = (
        jnp.dot(member, low, preferred_element_type=jnp.float32)
        + jnp.dot(member, middle, preferred_element_type=jnp.float32)
    ) + jnp.dot(member, high, preferred_element_type=jnp.float32)
    terms[...] = summed.reshape(terms.shape)

    def x_copy(step):
        to = other(l, step, layers)
        return remote(
            terms.at[:, to], from_layers.at[step - 1],
            x_send.at[step - 1], x_recv.at[step - 1], layer=to,
        )

    def s_copy(step):
        to = other(d, step, n)
        return remote(
            part.at[to], from_dp.at[step - 1], s_send.at[step - 1], s_recv.at[step - 1], dp=to
        )

    def r_copy(step):
        to = other(l, step, layers)
        return remote(
            total.at[l], total.at[l], r_send.at[step - 1], r_recv.at[step - 1], layer=to
        )

    for step in range(1, layers):
        x_copy(step).start()

    height = min(256, own_width)

    def add_block(own_of, col, first):
        def body(i, _):
            at = pl.ds(pl.multiple_of(i * height, LANES), height)
            block = lax.dot_general(
                own_of(i * height), col[...], (((0,), (0,)), ((), ())),
                preferred_element_type=jnp.float32,
            )
            acc[at] = block if first else acc[at] + block
            return 0

        lax.fori_loop(0, own_width // height, body, 0)

    add_block(
        lambda start: mv[:, pl.ds(pl.multiple_of(d * own_width + start, LANES), height)],
        mv.at[:, cols], True,
    )

    def over_layers():
        for step in range(1, layers):
            x_copy(step).wait_recv()
        value = terms[:, l]
        for step in range(1, layers):
            value = value + from_layers[step - 1]
        part[...] = value
        for step in range(1, n):
            s_copy(step).start()

    def over_dp():
        for step in range(1, n):
            s_copy(step).wait_recv()
        value = part[d]
        for step in range(1, n):
            value = value + from_dp[step - 1]
        total[l] = value
        for step in range(1, layers):
            r_copy(step).start()

    def f_copy(step, to_step):
        block = other(d, -step, n)
        return remote(
            ecol.at[block], eown.at[block], f_send.at[step - 1, to_step - 1], f_recv.at[step - 1],
            query=other(q, to_step, queries),
        )

    def exponents_on():
        for step in range(1, n):
            e_copy(step).wait_recv()

        @pl.when(q == source)
        def _():
            for step in range(1, n):
                for to_step in range(1, queries):
                    f_copy(step, to_step).start()

        @pl.when(q != source)
        def _():
            for step in range(1, n):
                f_copy(step, 1).wait_recv()

    core = lax.rem(q, 2)
    source_core = lax.rem(source, 2)
    sibling = q + 1 - 2 * core
    is_source = q == source
    is_relay = jnp.logical_and(q != source, core == source_core)

    def o_copy(way, step, c, k, from_source):
        block = incoming(way, step)
        at = pl.ds(c * piece, piece)
        src = gcol.at[block, at, own_in_col] if from_source else gown.at[block, at]
        to = sibling if k == 0 else other(q, 2 * k, queries)
        return remote(
            src, gown.at[block, at], o_send.at[way, step, c, k], o_recv.at[way, step, c], query=to
        )

    def on_arrival(way, step, c):
        @pl.when(arrives(way, step))
        def _():
            z_copy(way, step, c, False).wait_recv()

            @pl.when(sends(way, step + 1))
            def _():
                z_copy(way, step + 1, c, False).start()

            @pl.when(is_source)
            def _():
                for k in reversed(range(queries // 2)):
                    o_copy(way, step, c, k, True).start()

    last = jnp.where(d >= (n + 1) // 2, 0, n - 1)
    own_blocks = own_width // LANES

    def on_own(way, step, c):
        @pl.when(arrives(way, step))
        def _():
            block = incoming(way, step)
            at = pl.ds(c * piece, piece)
            here = slice(c * piece, (c + 1) * piece)
            scales = scale_columns(ecol[block])[here]
            for j in range(col_blocks):
                lanes = slice(j * LANES, (j + 1) * LANES)
                dcol[way, at, lanes] = gcol[block, at, lanes] * spread(scales[:, j:j + 1])

            def own_piece(source_ref, base):
                scales = scale_columns(
                    ecol[block] if source_ref is gcol else eown[block]
                )[here]
                lane = lax.broadcasted_iota(jnp.int32, scales.shape, 1)
                for j in range(own_blocks):
                    if own_blocks == col_blocks:
                        scale = scales[:, j:j + 1]
                    else:
                        chosen = lane == lax.div(offset, LANES) + j
                        scale = jnp.sum(jnp.where(chosen, scales, 0.0), axis=1, keepdims=True)
                    from_lanes = pl.ds(pl.multiple_of(base + j * LANES, LANES), LANES)
                    down[way, at, j * LANES:(j + 1) * LANES] = (
                        source_ref[block, at, from_lanes] * spread(scale)
                    )

            @pl.when(q == source)
            def _():
                own_piece(gcol, offset)

            @pl.when(q != source)
            def _():
                o_copy(way, step, c, 0, False).wait_recv()

                @pl.when(is_relay)
                def _():
                    o_copy(way, step, c, 0, False).start()

                own_piece(gown, 0)

            @pl.when(block == last)
            def _():
                col_out[at] = dcol[way, at]
                own_out[at] = down[way, at]

            if c == pieces - 1:
                @pl.when(block != last)
                def _():
                    add_block(
                        lambda start: down[way, :, pl.ds(pl.multiple_of(start, LANES), height)],
                        dcol.at[way], False,
                    )

    items = [(way, step, c) for step in range(n - 1) for c in range(pieces) for way in (0, 1)]
    lag = 4
    for i in range(len(items) + lag):
        if i < len(items):
            on_arrival(*items[i])
        if i >= lag:
            on_own(*items[i - lag])
        if i == 1:
            exponents_on()
        if i == 3:
            over_layers()
        if i == len(items) * 2 // 3:
            over_dp()

    for step in range(1, layers):
        r_copy(step).wait_recv()
    ds_out[...] = total[...]

    @pl.when(q == source)
    def _():
        for step in range(1, n):
            for to_step in range(1, queries):
                f_copy(step, to_step).wait_send()

    for step in range(1, n):
        e_copy(step).wait_send()
        s_copy(step).wait_send()
    for step in range(1, layers):
        x_copy(step).wait_send()
        r_copy(step).wait_send()
    for way, step, c in items:
        @pl.when(sends(way, step))
        def _(way=way, step=step, c=c):
            z_copy(way, step, c, step == 0).wait_send()

        @pl.when(jnp.logical_and(arrives(way, step), is_source))
        def _(way=way, step=step, c=c):
            for k in range(queries // 2):
                o_copy(way, step, c, k, True).wait_send()

        @pl.when(jnp.logical_and(arrives(way, step), is_relay))
        def _(way=way, step=step, c=c):
            o_copy(way, step, c, 0, False).wait_send()


def fisher_kernel(scale, acc, col, own, ds_in, fisher, ds_out, tile, t_sem, ds_sem):
    ds_copy = pltpu.make_async_copy(ds_in, ds_out, ds_sem)
    ds_copy.start()
    steps, height, _ = tile.shape

    def t_copy(i):
        return pltpu.make_async_copy(
            tile.at[i], fisher.at[0, pl.ds(pl.multiple_of(i * height, 8), height)], t_sem.at[i]
        )

    def body(i, _):
        at = pl.ds(pl.multiple_of(i * height, LANES), height)
        block = lax.dot_general(
            own[:, at], col[...], (((0,), (0,)), ((), ())), preferred_element_type=jnp.float32
        )
        tile[i] = (acc[at] + block) * scale
        t_copy(i).start()
        return 0

    lax.fori_loop(0, steps, body, 0)
    for i in range(steps):
        t_copy(i).wait()
    ds_copy.wait()


def per_device(mantissas, exponents, queries, doc_ids, owners):
    n, layers, nq = (lax.axis_size(a) for a in ("dp", "layer", "query"))
    rows, _, width = mantissas.shape
    m = mantissas.reshape(rows, width)
    e = jnp.transpose(exponents[:, 0, :])
    qs = queries.reshape(queries.shape[0], width)
    docs = owners.shape[0]
    own_width, col_width = width // n, width // nq
    col_blocks = col_width // LANES
    slots = docs // n
    sub = slots // layers
    pieces = max(1, 16 // n)
    count = qs.shape[0]
    f32, bf16 = jnp.float32, jnp.bfloat16
    dma = pltpu.SemaphoreType.DMA
    anyspace = pl.BlockSpec(memory_space=pl.ANY)
    vmem = pl.BlockSpec(memory_space=pltpu.VMEM)
    hbm = pl.BlockSpec(memory_space=pltpu.HBM)
    acc, col, own, ds = pl.pallas_call(
        functools.partial(gather_kernel, (n, layers, nq, pieces, own_width)),
        out_shape=(
            pltpu.VMEM((own_width, col_width), f32),
            pltpu.VMEM((rows, col_width), bf16),
            pltpu.VMEM((rows, own_width), bf16),
            pltpu.VMEM((layers, sub, count), f32),
        ),
        in_specs=[hbm] * 5,
        out_specs=(vmem, vmem, vmem, vmem),
        scratch_shapes=[
            pltpu.VMEM((n, rows, col_width), bf16),
            pltpu.VMEM((n, rows, own_width), bf16),
            pltpu.VMEM((n, col_blocks, rows), jnp.int32),
            pltpu.VMEM((n, col_blocks, rows), jnp.int32),
            pltpu.VMEM((2, rows, col_width), bf16),
            pltpu.VMEM((2, rows, own_width), bf16),
            pltpu.VMEM((rows, width), bf16),
            pltpu.VMEM((count, width), bf16),
            pltpu.VMEM(e.shape, jnp.int32),
            pltpu.VMEM((1, rows), jnp.int32),
            pltpu.VMEM((1, docs), jnp.int32),
            pltpu.VMEM((n, layers, sub, count), f32),
            pltpu.VMEM((layers - 1, n, sub, count), f32),
            pltpu.VMEM((n, sub, count), f32),
            pltpu.VMEM((n - 1, sub, count), f32),
            pltpu.VMEM((layers, sub, count), f32),
            dma((5,)),
            dma((2, n - 1, pieces)),
            dma((2, n - 1, pieces)),
            dma((2, n - 1, pieces, nq // 2)),
            dma((2, n - 1, pieces)),
            dma((n - 1,)),
            dma((n - 1,)),
            dma((n - 1, nq - 1)),
            dma((n - 1,)),
            dma((layers - 1,)),
            dma((layers - 1,)),
            dma((n - 1,)),
            dma((n - 1,)),
            dma((layers - 1,)),
            dma((layers - 1,)),
        ],
        compiler_params=pltpu.CompilerParams(
            collective_id=0, has_side_effects=True, vmem_limit_bytes=58 * 2**20
        ),
        name="gather",
    )(m, e, qs, doc_ids.reshape(1, rows), owners.reshape(1, docs))
    height = min(256, own_width)
    steps = own_width // height
    fisher, ds = pl.pallas_call(
        functools.partial(fisher_kernel, 1.0 / (n * rows)),
        out_shape=(
            jax.ShapeDtypeStruct((1, own_width, col_width), f32),
            jax.ShapeDtypeStruct((layers, sub, count), f32),
        ),
        in_specs=[vmem] * 4,
        out_specs=(hbm, hbm),
        scratch_shapes=[
            pltpu.VMEM((steps, height, col_width), f32),
            dma((steps,)),
            dma,
        ],
        compiler_params=pltpu.CompilerParams(vmem_limit_bytes=16 * 2**20),
        name="fisher",
    )(acc, col, own, ds)
    return fisher, ds.reshape(slots, count)


def solution(mesh):
    in_specs = (
        P("dp", "layer", None),
        P("dp", "layer", None),
        P("query", "layer", None),
        P("dp"),
        P(),
    )
    out_specs = (P("layer", "dp", "query"), P("dp", "query"))
    return jax.shard_map(
        per_device, mesh=mesh, in_specs=in_specs, out_specs=out_specs, check_vma=False
    )
```
